256 devices in a mesh: gx: 64 (over z, x, core), gz: 4 (over y).
Axes of the slice: x: 4, y: 4, z: 8, core: 2. Of those that a mesh axis runs over, the one named last changes fastest.
Arguments:
- velocity: float32 [3, 2048, 256, 128], P(None, 'gx', 'gz'), may hold values from -6 to 6
- rhs_old: float32 [3, 2048, 256, 128], P(None, 'gx', 'gz'), may hold values from -6 to 6
Outputs:
- velocity_next: float32 [3, 2048, 256, 128], P(None, 'gx', 'gz')
- convective: float32 [3, 2048, 256, 128], P(None, 'gx', 'gz')
The draws below stay inside these ranges and needn't reach their ends.
All inputs are finite; a program needn't handle non-finite values.
Results may differ from the reference program's by a relative error of at most 0.00018.
Values sent between devices are 32-bit elements; how exact they have to be, the bound alone decides.
A program may use at most 128 MiB of HBM per device.

```python
import jax
import jax.numpy as jnp
from jax import lax

CY = 128
NX = 2048
NZ = 256
FILT = 512


def draw_velocity(key, part):
    subkeys = jax.random.split(jax.random.fold_in(key, 7), 3)
    extent = (3, NX, NZ, CY)
    position = jnp.arange(NX, dtype=jnp.float32) / NX
    amplitude = jax.random.uniform(subkeys[1], (3, 3, 1, NZ, CY), jnp.float32, 0.5, 1.5)
    phase_shift = jax.random.uniform(subkeys[2], (3, 3, 1, NZ, CY), jnp.float32, -jnp.pi, jnp.pi)
    wave_sum = jnp.zeros(extent, jnp.float32)
    for harmonic in range(3):
        phase_arg = 2.0 * jnp.pi * (harmonic + 1) * position[None, :, None, None] + phase_shift[harmonic]
        wave_sum = wave_sum + amplitude[harmonic] * jnp.sin(phase_arg) / (harmonic + 1)
    irregular = 0.7 * jax.random.truncated_normal(subkeys[0], -4.0, 4.0, extent, jnp.float32)
    mean_flow = jnp.array([1.0, 0.0, 0.4], jnp.float32).reshape(3, 1, 1, 1)
    return irregular + mean_flow + 0.5 * wave_sum


def shard_levels(rng, dims, cuts, low, top_value):
    def one(dim, shards_of):
        draws = jax.random.uniform(jax.random.fold_in(jax.random.fold_in(rng, 6), dim), (shards_of,), jnp.float32, low / len(cuts), top_value / len(cuts))
        return jnp.repeat(jnp.exp(draws), dims[dim] // shards_of).reshape((-1,) + (1,) * (len(dims) - dim - 1))

    factor_of = one(*cuts[0])
    for cut in cuts[1:]:
        factor_of = factor_of * one(*cut)
    return factor_of


def normal_values(stream_key, shape, scale, bound, cuts=(), held_as=jnp.bfloat16):
    level = shard_levels(stream_key, shape, cuts, -0.22, 0.18) if cuts else 1.0
    values = jax.random.normal(stream_key, shape, jnp.float32) * scale * level
    return jnp.minimum(jnp.maximum(values, -bound), bound).astype(held_as)


def setup_inputs(seed: int = 0) -> dict:
    key_list = jax.random.split(jax.random.key(seed), 3)
    velocity = draw_velocity(jax.random.fold_in(key_list[2], 71), 0)
    rhs_old = normal_values(key_list[1], (3, NX, NZ, CY), 1.0, 6.0, ((1, 64), (2, 4)), jnp.float32)
    return dict(velocity=velocity, rhs_old=rhs_old)


def gradients(field):
    along = 45.0 * (jnp.roll(field, -1, 0) - jnp.roll(field, 1, 0))
    along = along - 9.0 * (jnp.roll(field, -2, 0) - jnp.roll(field, 2, 0))
    along = (along + (jnp.roll(field, -3, 0) - jnp.roll(field, 3, 0))) / 60.0
    span = 45.0 * (jnp.roll(field, -1, 1) - jnp.roll(field, 1, 1))
    span = span - 9.0 * (jnp.roll(field, -2, 1) - jnp.roll(field, 2, 1))
    span = (span + (jnp.roll(field, -3, 1) - jnp.roll(field, 3, 1))) / 60.0
    return along, span


def filtered(field):
    count = field.shape[0]
    wave = 2.0 * jnp.pi * jnp.arange(count, dtype=field.dtype) / count
    strength = 1.0 * FILT * FILT
    symbol = 1.0 + 4.0 * strength * jnp.sin(0.5 * wave) ** 2
    spectrum = jnp.fft.fft(field, axis=0) / symbol[:, None, None]
    return jnp.real(jnp.fft.ifft(spectrum, axis=0)).astype(field.dtype)


def reference(velocity, rhs_old):
    along, span = lax.map(gradients, velocity)
    smooth = lax.map(filtered, velocity[0::2])
    convective = -(smooth[0:1] * along + smooth[1:2] * span)
    velocity_next = velocity + 0.5 * ((5.0 / 12.0) * convective - (17.0 / 60.0) * rhs_old)
    return velocity_next, convective
```

```python
import functools
import math

import jax
import jax.numpy as jnp
from jax import lax
from jax.experimental import pallas as pl
from jax.experimental.pallas import tpu as pltpu
from jax.sharding import PartitionSpec as P

MESH = pl.DeviceIdType.MESH
ROW = 8
HALO = 3
PAD = 8


def constants(cx, blocks):
    filter_cells = cx * blocks // 4
    coupling = 1.0 * filter_cells * filter_cells
    theta = 2.0 * math.asinh(0.5 / math.sqrt(coupling))
    ratio = math.exp(-theta)
    gain = 1.0 / (coupling * 2.0 * math.sinh(theta))
    return ratio, gain


def gather_kernel(
    cx, cz, groups, lines,
    v_hbm, rhs_hbm,
    along_ref, span_ref, base_ref, local_ref, pq_ref,
    vpad, rhs, ends, recv_row, total, recv_group, back, recv_back, zsend, zrecv,
    load_sem, send_row, got_row, send_group, got_group, send_back, got_back,
    send_x, got_x, send_z, got_z,
):
    blocks = groups * ROW
    ratio, gain = constants(cx, blocks)
    me = lax.axis_index("gx")
    my_line = lax.axis_index("gz")
    spot = lax.rem(me, ROW)
    group = lax.div(me, ROW)
    top = PAD
    bottom = PAD + cz

    def at(gx, gz=None):
        return {"gx": gx, "gz": my_line if gz is None else gz}

    loads = []
    for comp in (0, 2, 1):
        copy = pltpu.make_async_copy(
            v_hbm.at[comp], vpad.at[comp, pl.ds(HALO, cx), pl.ds(PAD, cz), :], load_sem.at[comp]
        )
        copy.start()
        loads.append(copy)
    rhs_load = pltpu.make_async_copy(rhs_hbm, rhs, load_sem.at[3])
    rhs_load.start()

    row_peers = [group * ROW + lax.rem(spot + d, ROW) for d in range(1, ROW)]
    group_peers = [lax.rem(group + d, groups) * ROW + spot for d in range(1, groups)]
    right = lax.rem(me + 1, blocks)
    left = lax.rem(me + blocks - 1, blocks)
    above = lax.rem(my_line + 1, lines)
    below = lax.rem(my_line + lines - 1, lines)
    barrier = pltpu.get_barrier_semaphore()
    friends = [at(g) for g in row_peers + group_peers + [right, left]]
    friends += [at(me, above), at(me, below)]
    for friend in friends:
        pl.semaphore_signal(barrier, inc=1, device_id=friend, device_id_type=MESH)

    def plane(comp, i):
        return vpad[comp, HALO + i, PAD : PAD + cz, :]

    for mode in range(2):
        loads[mode].wait()
        comp = 2 * mode
        forward = plane(comp, 0)
        backward = forward
        for i in range(1, cx):
            value = plane(comp, i)
            forward = value + ratio * forward
            backward = backward + (ratio**i) * value
        for k in range(ROW):
            ends[k, mode] = forward[8 * k : 8 * k + 8]
            ends[k, 2 + mode] = backward[8 * k : 8 * k + 8]
    loads[2].wait()

    pl.semaphore_wait(barrier, len(friends))

    def send(src, dst, sent, got, device):
        copy = pltpu.make_async_remote_copy(
            src_ref=src, dst_ref=dst, send_sem=sent, recv_sem=got, device_id=device, device_id_type=MESH
        )
        copy.start()
        return copy

    row_copies = []
    for d in range(1, ROW):
        peer = lax.rem(spot + d, ROW)
        row_copies.append(
            send(ends.at[peer], recv_row.at[spot], send_row.at[d], got_row.at[d], at(row_peers[d - 1]))
        )
    recv_row[spot] = ends[spot]

    flat = vpad.reshape(3 * (cx + 2 * HALO) * (cz + 2 * PAD), 128)
    tall = cz + 2 * PAD

    def strided(comp, row):
        start = (comp * (cx + 2 * HALO) + HALO) * tall + row
        return pl.ds(start, cx, stride=tall)

    for comp in range(3):
        for k in range(HALO):
            zsend[0, 3 * comp + k] = flat[strided(comp, PAD + k), :]
            zsend[1, 3 * comp + k] = flat[strided(comp, PAD + cz - HALO + k), :]
    z_copies = [
        send(zsend.at[0], zrecv.at[1], send_z.at[0], got_z.at[0], at(me, below)),
        send(zsend.at[1], zrecv.at[0], send_z.at[1], got_z.at[1], at(me, above)),
    ]
    body_rows = pl.ds(PAD, cz)
    x_copies = [
        send(
            vpad.at[:, pl.ds(HALO, HALO), body_rows, :],
            vpad.at[:, pl.ds(HALO + cx, HALO), body_rows, :],
            send_x.at[0], got_x.at[0], at(left),
        ),
        send(
            vpad.at[:, pl.ds(cx, HALO), body_rows, :],
            vpad.at[:, pl.ds(0, HALO), body_rows, :],
            send_x.at[1], got_x.at[1], at(right),
        ),
    ]

    for copy in row_copies:
        copy.wait_recv()
    jump = ratio**cx
    fwd = recv_row[0, 0:2]
    bwd = recv_row[ROW - 1, 2:4]
    for i in range(1, ROW):
        fwd = recv_row[i, 0:2] + jump * fwd
        bwd = recv_row[ROW - 1 - i, 2:4] + jump * bwd
    total[0:2] = fwd
    total[2:4] = bwd
    recv_group[group, 0:2] = fwd
    recv_group[group, 2:4] = bwd
    group_copies = []
    for d in range(1, groups):
        group_copies.append(
            send(total, recv_group.at[group], send_group.at[d], got_group.at[d], at(group_peers[d - 1]))
        )

    def local_step(mode, comp):
        state = jnp.zeros((cz, 128), jnp.float32)

        def up(i, state):
            state = vpad[comp, HALO + i, top:bottom, :] + ratio * state
            local_ref[mode, i] = state
            return state

        lax.fori_loop(0, cx, up, state)

        def down(n, state):
            i = cx - 1 - n
            local_ref[mode, i] = (-gain) * (local_ref[mode, i] + state)
            return ratio * (vpad[comp, HALO + i, top:bottom, :] + state)

        lax.fori_loop(0, cx, down, state)

    local_step(0, 0)
    local_step(1, 2)
    rhs_load.wait()

    for copy in x_copies:
        copy.wait()

    def along_step(i, carry):
        for comp in range(3):
            near = vpad[comp, i + 4, top:bottom, :] - vpad[comp, i + 2, top:bottom, :]
            mid = vpad[comp, i + 5, top:bottom, :] - vpad[comp, i + 1, top:bottom, :]
            far = vpad[comp, i + 6, top:bottom, :] - vpad[comp, i, top:bottom, :]
            along_ref[comp, i] = (45.0 / 60.0) * near - (9.0 / 60.0) * mid + (1.0 / 60.0) * far
            base_ref[comp, i] = vpad[comp, i + 3, top:bottom, :] - (0.5 * 17.0 / 60.0) * rhs[comp, i]
        return carry

    lax.fori_loop(0, cx, along_step, 0)

    for copy in group_copies:
        copy.wait_recv()
    wide = jump**ROW
    closing = 1.0 / (1.0 - wide**groups)
    inflow = recv_group[group, 0:2]
    outflow = recv_group[group, 2:4]
    for d in range(1, groups):
        inflow = recv_group[lax.rem(group + d, groups), 0:2] + wide * inflow
        outflow = recv_group[lax.rem(group + groups - d, groups), 2:4] + wide * outflow
    inflow = closing * inflow
    outflow = closing * outflow
    for i in range(ROW):
        back[i, 0:2] = inflow
        back[ROW - 1 - i, 2:4] = outflow
        inflow = recv_row[i, 0:2] + jump * inflow
        outflow = recv_row[ROW - 1 - i, 2:4] + jump * outflow
    back_copies = []
    for d in range(1, ROW):
        peer = lax.rem(spot + d, ROW)
        back_copies.append(
            send(back.at[peer], recv_back.at[spot], send_back.at[d], got_back.at[d], at(row_peers[d - 1]))
        )
    recv_back[spot] = back[spot]

    for copy in z_copies:
        copy.wait()
    for comp in range(3):
        for k in range(HALO):
            flat[strided(comp, PAD - HALO + k), :] = zrecv[0, 3 * comp + k]
            flat[strided(comp, PAD + cz + k), :] = zrecv[1, 3 * comp + k]

    def span_step(i, carry):
        for comp in range(3):
            def shifted(s):
                return vpad[comp, i + HALO, top + s : bottom + s, :]

            near = shifted(1) - shifted(-1)
            mid = shifted(2) - shifted(-2)
            far = shifted(3) - shifted(-3)
            span_ref[comp, i] = (45.0 / 60.0) * near - (9.0 / 60.0) * mid + (1.0 / 60.0) * far
        return carry

    lax.fori_loop(0, cx, span_step, 0)

    for copy in back_copies:
        copy.wait_recv()
    pq_ref[...] = recv_back[...]
    for copy in row_copies + group_copies + back_copies:
        copy.wait_send()


def finish_kernel(
    cx, cz, blocks, along_ref, span_ref, base_ref, local_ref, pq_ref, next_hbm, conv_hbm, nxt, conv, sem
):
    ratio, gain = constants(cx, blocks)
    steps = 8
    per = cx // steps
    copies = []
    for step in range(steps):
        for k in range(ROW):
            rows = slice(8 * k, 8 * k + 8)
            edges = [pq_ref[k, n] for n in range(4)]
            for i in range(step * per, step * per + per):
                rise = -gain * ratio ** (i + 1)
                fall = -gain * ratio ** (cx - i)
                smooth = [
                    local_ref[m, i, rows, :] + (rise * edges[m] + fall * edges[2 + m]) for m in range(2)
                ]
                for comp in range(3):
                    value = smooth[0] * along_ref[comp, i, rows, :] + smooth[1] * span_ref[comp, i, rows, :]
                    conv[comp, i, rows, :] = value
                    nxt[comp, i, rows, :] = base_ref[comp, i, rows, :] + (0.5 * 5.0 / 12.0) * value
        part = pl.ds(step * per, per)
        for n, (src, dst) in enumerate(((nxt, next_hbm), (conv, conv_hbm))):
            copy = pltpu.make_async_copy(src.at[:, part], dst.at[:, part], sem.at[n, step])
            copy.start()
            copies.append(copy)
    for copy in copies:
        copy.wait()


def per_device(velocity, rhs_old, blocks, lines):
    _, cx, cz, lanes = velocity.shape
    groups = blocks // ROW
    f32 = jnp.float32
    field = (3, cx, cz, lanes)
    piece = (4, 8, lanes)
    dma = pltpu.SemaphoreType.DMA
    hbm = pl.BlockSpec(memory_space=pltpu.MemorySpace.HBM)
    vmem = pl.BlockSpec(memory_space=pltpu.MemorySpace.VMEM)
    shapes = [field, field, field, (2, cx, cz, lanes), (ROW,) + piece]
    parts = pl.pallas_call(
        functools.partial(gather_kernel, cx, cz, groups, lines),
        out_shape=[pltpu.VMEM(s, f32) for s in shapes],
        in_specs=[hbm, hbm],
        out_specs=[vmem] * 5,
        scratch_shapes=[
            pltpu.VMEM((3, cx + 2 * HALO, cz + 2 * PAD, lanes), f32),
            pltpu.VMEM(field, f32),
            pltpu.VMEM((ROW,) + piece, f32),
            pltpu.VMEM((ROW,) + piece, f32),
            pltpu.VMEM(piece, f32),
            pltpu.VMEM((groups,) + piece, f32),
            pltpu.VMEM((ROW,) + piece, f32),
            pltpu.VMEM((ROW,) + piece, f32),
            pltpu.VMEM((2, 9, cx, lanes), f32),
            pltpu.VMEM((2, 9, cx, lanes), f32),
            dma((4,)), dma((ROW,)), dma((ROW,)), dma((groups,)), dma((groups,)), dma((ROW,)), dma((ROW,)),
            dma((2,)), dma((2,)), dma((2,)), dma((2,)),
        ],
        compiler_params=pltpu.CompilerParams(
            collective_id=0, has_side_effects=True, vmem_limit_bytes=24 << 20
        ),
        name="gather",
    )(velocity, rhs_old)
    return pl.pallas_call(
        functools.partial(finish_kernel, cx, cz, blocks),
        out_shape=[jax.ShapeDtypeStruct(field, f32)] * 2,
        in_specs=[vmem] * 5,
        out_specs=[hbm, hbm],
        scratch_shapes=[pltpu.VMEM(field, f32), pltpu.VMEM(field, f32), dma((2, 8))],
        compiler_params=pltpu.CompilerParams(vmem_limit_bytes=24 << 20),
        name="finish",
    )(*parts)


def solution(mesh):
    placed = (P(None, "gx", "gz", None), P(None, "gx", "gz", None))

    def call(velocity, rhs_old):
        return tuple(per_device(velocity, rhs_old, mesh.shape["gx"], mesh.shape["gz"]))

    return jax.shard_map(
        call,
        mesh=mesh,
        in_specs=placed,
        out_specs=placed,
        check_vma=False,
    )
```
